32 devices in a mesh: row: 8 (over y, x, core), col: 4 (over z).
Axes of the slice: x: 2, y: 2, z: 4, core: 2. Of those that a mesh axis runs over, the one named last changes fastest.
Arguments:
- amplitudes: bfloat16 [2048, 8192], P('row', 'col'), may hold values from -0.125 to 0.125
- integrals: bfloat16 [8192, 1024], P('col', 'row'), may hold values from -6 to 6
- occ_irrep: int32 [200], replicated, may hold values from 0 to 3
- vir_irrep: int32 [6], replicated, may hold values from 0 to 3
- occ_energy: float32 [200], replicated, may hold values from -1 to -0.3
- vir_energy: float32 [1536], replicated, may hold values from 0.2 to 1.5
Outputs:
- update: float32 [2048, 1024], P('row', 'col')
The draws below stay inside these ranges and needn't reach their ends.
All inputs are finite; a program needn't handle non-finite values.
Results may differ from the reference program's by a relative error of at most 0.0003.
Values may be sent and summed in bfloat16 or wider, within the bound.
A program may use at most 128 MiB of HBM per device.

```python
import jax
import jax.numpy as jnp
from jax import lax

NV = 1536
NOCC = 200
TILE = 256
NIRR = 4
NVT = 6
P_ROWS = 2048
K_COLS = 8192
Q_COLS = 1024


def with_ends(values, rng, least, top_value):
    longest = values.shape.index(max(values.shape))
    spots = []
    for shift in (0, 1):
        where = [jax.random.randint(jax.random.fold_in(rng, axis), (), 0, length) for axis, length in enumerate(values.shape)]
        where[longest] = (where[longest] + shift) % values.shape[longest]
        spots.append(tuple(where))
    return values.at[spots[0]].set(least).at[spots[1]].set(top_value)


def steps_of(own_key, extent, shards, smallest, top_value):
    def one(position, shards_of):
        heights = jax.random.uniform(jax.random.fold_in(jax.random.fold_in(own_key, 6), position), (shards_of,), jnp.float32, smallest / len(shards), top_value / len(shards))
        return jnp.repeat(jnp.exp(heights), extent[position] // shards_of).reshape((-1,) + (1,) * (len(extent) - position - 1))

    gain = one(*shards[0])
    for cut in shards[1:]:
        gain = gain * one(*cut)
    return gain


def noise(rng, dims, deviation, most, pieces=(), kind=jnp.bfloat16):
    factor_of = steps_of(rng, dims, pieces, -0.22, 0.18) if pieces else 1.0
    result = jax.random.normal(rng, dims, jnp.float32) * deviation * factor_of
    return jnp.minimum(jnp.maximum(result, -most), most).astype(kind)


def setup_inputs(seed: int = 0) -> dict:
    seeds = jax.random.split(jax.random.key(seed), 7)
    amplitudes = noise(seeds[0], (P_ROWS, K_COLS), (K_COLS // NIRR) ** -0.5, 0.125, ((0, 8), (1, 4)))
    integrals = noise(seeds[1], (K_COLS, Q_COLS), 1.0, 6.0, ((0, 4), (1, 8)))
    occ_irrep = with_ends(jax.random.randint(seeds[2], (NOCC,), 0, NIRR), jax.random.fold_in(seeds[2], 1), 0, NIRR - 1).astype(jnp.int32)
    vir_irrep = with_ends(jax.random.randint(seeds[3], (NVT,), 0, NIRR), jax.random.fold_in(seeds[3], 1), 0, NIRR - 1).astype(jnp.int32)
    occ_energy = jnp.clip(jax.random.uniform(seeds[4], (NOCC,), jnp.float32, -1.0, -0.3), -1.0, -0.3)
    vir_energy = jnp.clip(jax.random.uniform(seeds[5], (NV,), jnp.float32, 0.2, 1.5), 0.2, 1.5)
    return {"amplitudes": amplitudes, "integrals": integrals, "occ_irrep": occ_irrep, "vir_irrep": vir_irrep, "occ_energy": occ_energy, "vir_energy": vir_energy}


def irreps(count, occ_irrep, vir_irrep):
    tiles = jnp.arange(count, dtype=jnp.int32)
    return jnp.bitwise_xor(occ_irrep[tiles // NVT], vir_irrep[tiles % NVT])


def masked(matrix, row_irr, col_irr):
    keep = (row_irr[:, None] == col_irr[None, :]).astype(jnp.float32)
    rows, cols = matrix.shape
    blocks = matrix.astype(jnp.float32).reshape(rows // TILE, TILE, cols // TILE, TILE)
    return (blocks * keep[:, None, :, None]).reshape(rows, cols)


def pair_energy(count, occ_energy, vir_energy):
    index = jnp.arange(count, dtype=jnp.int32)
    return vir_energy[index % NV] - occ_energy[index // NV]


def reference(amplitudes, integrals, occ_irrep, vir_irrep, occ_energy, vir_energy):
    p_irr = irreps(P_ROWS // TILE, occ_irrep, vir_irrep)
    k_irr = irreps(K_COLS // TILE, occ_irrep, vir_irrep)
    q_irr = irreps(Q_COLS // TILE, occ_irrep, vir_irrep)
    masked_amp = masked(amplitudes, p_irr, k_irr)
    masked_int = masked(integrals, k_irr, q_irr)
    cycle = jnp.dot(masked_amp, masked_int, precision=lax.Precision.HIGHEST, preferred_element_type=jnp.float32)
    denom = pair_energy(P_ROWS, occ_energy, vir_energy)[:, None] + pair_energy(Q_COLS, occ_energy, vir_energy)[None, :]
    return cycle / denom
```

```python
import functools

import jax
import jax.numpy as jnp
from jax import lax
from jax.experimental import pallas as pl
from jax.experimental.pallas import tpu as pltpu
from jax.sharding import PartitionSpec as P

TILE = 256
MESH = pl.DeviceIdType.MESH


def lookup(table, index):
    hits = index[:, None] == jnp.arange(table.shape[0], dtype=jnp.int32)[None, :]
    return jnp.sum(jnp.where(hits, table[None, :], jnp.zeros_like(table)[None, :]), axis=1)


def irreps(first_tile, count, occ_irrep, vir_irrep, tiles_virtual):
    tiles = first_tile + jnp.arange(count, dtype=jnp.int32)
    return jnp.bitwise_xor(
        lookup(occ_irrep, tiles // tiles_virtual), lookup(vir_irrep, tiles % tiles_virtual)
    )


def general(amplitudes, integrals, occ_irrep, vir_irrep, occ_energy, vir_energy):
    tile_size = TILE
    tiles_virtual = vir_irrep.shape[0]
    virtual_count = vir_energy.shape[0]
    p_rows, k_cols = amplitudes.shape
    p_tiles = p_rows // tile_size
    k_tiles = k_cols // tile_size
    row_index = lax.axis_index("row")
    col_index = lax.axis_index("col")
    p_irr = irreps(row_index * p_tiles, p_tiles, occ_irrep, vir_irrep, tiles_virtual)
    k_irr = irreps(col_index * k_tiles, k_tiles, occ_irrep, vir_irrep, tiles_virtual)
    match = p_irr[:, None] == k_irr[None, :]
    masked_amp = (
        amplitudes.reshape(p_tiles, tile_size, k_tiles, tile_size)
        * match[:, None, :, None].astype(jnp.bfloat16)
    ).reshape(p_rows, k_cols)
    piece = lax.all_gather(integrals, "row", axis=1, tiled=True)
    width = piece.shape[1]
    columns = jnp.arange(width, dtype=jnp.int32)
    column_tiles = columns // tile_size
    q_irr = jnp.bitwise_xor(
        lookup(occ_irrep, column_tiles // tiles_virtual),
        lookup(vir_irrep, column_tiles % tiles_virtual),
    )
    keeper = (k_irr[:, None] == q_irr[None, :]).astype(jnp.bfloat16)
    masked_int = (piece.reshape(k_tiles, tile_size, width) * keeper[:, None, :]).reshape(
        k_cols, width
    )
    partial_cycle = jnp.dot(masked_amp, masked_int, preferred_element_type=jnp.float32)
    cycle = lax.psum_scatter(partial_cycle, "col", scatter_dimension=1, tiled=True)
    q_cols = cycle.shape[1]
    row_pairs = row_index * p_rows + jnp.arange(p_rows, dtype=jnp.int32)
    col_pairs = col_index * q_cols + jnp.arange(q_cols, dtype=jnp.int32)
    row_energy = lookup(vir_energy, row_pairs % virtual_count) - lookup(
        occ_energy, row_pairs // virtual_count
    )
    col_energy = lookup(vir_energy, col_pairs % virtual_count) - lookup(
        occ_energy, col_pairs // virtual_count
    )
    return cycle / (row_energy[:, None] + col_energy[None, :])


CHUNKS = 4
SPLITS = 2
COLS = 128


def cycle_kernel(
    nz,
    amp_hbm,
    int_hbm,
    occ_irr,
    vir_irr,
    occ_e,
    vir_e,
    out_ref,
    blocks,
    amp,
    part,
    incoming,
    denom,
    local_sem,
    near_send,
    near_recv,
    fwd_send,
    sib_send,
    sib_recv,
    z_send,
    z_recv,
):
    r = lax.axis_index("row")
    z = lax.axis_index("col")
    core = r % 2
    x = (r // 2) % 2
    y = r // 4
    xr = r + 2 - 4 * x
    yr = r + 4 - 8 * y
    dr = xr + yr - r
    shift = 1 - 2 * core
    sr = r + shift
    rows_of = (r, xr, yr, dr)
    depth = int_hbm.shape[0]
    step = depth // CHUNKS
    height = TILE // SPLITS
    tiles_virtual = vir_irr.shape[0]
    k_tiles = depth // TILE

    int_copy = pltpu.make_async_copy(int_hbm, blocks.at[r], local_sem.at[0])
    int_copy.start()
    amp_copy = pltpu.make_async_copy(amp_hbm, amp, local_sem.at[1])
    amp_copy.start()

    barrier = pltpu.get_barrier_semaphore()
    for target in (xr, yr, sr):
        pl.semaphore_signal(barrier, inc=1, device_id=(target, z), device_id_type=MESH)

    @pl.when(z > 0)
    def _():
        pl.semaphore_signal(barrier, inc=1, device_id=(r, z - 1), device_id_type=MESH)

    @pl.when(z < nz - 1)
    def _():
        pl.semaphore_signal(barrier, inc=1, device_id=(r, z + 1), device_id_type=MESH)

    ends = jnp.where(z > 0, 1, 0) + jnp.where(z < nz - 1, 1, 0)
    pl.semaphore_wait(barrier, 3 + ends)

    def at(ref, chunk):
        return ref.at[pl.ds(chunk * step, step)]

    def remote(src, dst, send_sem, recv_sem, target):
        return pltpu.make_async_remote_copy(
            src_ref=src,
            dst_ref=dst,
            send_sem=send_sem,
            recv_sem=recv_sem,
            device_id=target,
            device_id_type=MESH,
        )

    half = CHUNKS // 2
    x_order = list(range(CHUNKS))
    y_order = x_order[half:] + x_order[:half]

    def near(axis, chunk):
        return remote(
            at(int_hbm, chunk),
            at(blocks.at[r], chunk),
            near_send.at[axis, chunk],
            near_recv.at[axis, chunk],
            ((xr, yr)[axis], z),
        )

    def arrival(rel, chunk):
        ref = at(blocks.at[rows_of[rel]], chunk)
        return remote(ref, ref, near_send.at[0, chunk], near_recv.at[rel - 1, chunk], (xr, z))

    def forward(chunk):
        source, target = (xr, yr) if chunk < half else (yr, xr)
        ref = at(blocks.at[source], chunk)
        return remote(ref, ref, fwd_send.at[chunk], near_recv.at[2, chunk], (target, z))

    def to_sibling(rel, chunk):
        source = rows_of[rel]
        src = at(int_hbm, chunk) if rel == 0 else at(blocks.at[source], chunk)
        return remote(
            src,
            at(blocks.at[source], chunk),
            sib_send.at[rel, chunk],
            sib_recv.at[rel, chunk],
            (sr, z),
        )

    def sibling_arrival(rel, chunk):
        ref = at(blocks.at[rows_of[rel] + shift], chunk)
        return remote(ref, ref, sib_send.at[rel, chunk], sib_recv.at[rel, chunk], (sr, z))

    for cx, cy in zip(x_order, y_order):
        near(0, cx).start()
        near(1, cy).start()
    for chunk in range(CHUNKS):
        to_sibling(0, chunk).start()

    v_row = vir_e[:, pl.ds(pl.multiple_of((r % tiles_virtual) * TILE, TILE), TILE)]
    v_col = vir_e[:, pl.ds(pl.multiple_of((z % tiles_virtual) * TILE, TILE), TILE)]
    row_energy = v_row - occ_e[r // tiles_virtual]
    col_energy = v_col - occ_e[z // tiles_virtual]
    denom[...] = jnp.broadcast_to(row_energy, (TILE, TILE)).T + col_energy

    p_irr = occ_irr[r // tiles_virtual] ^ vir_irr[r % tiles_virtual]
    q_irr = occ_irr[z // tiles_virtual] ^ vir_irr[z % tiles_virtual]
    keep = jnp.where(p_irr == q_irr, 1.0, 0.0).astype(jnp.float32)

    amp_copy.wait()
    for tile in range(k_tiles):
        number = z * k_tiles + tile
        k_irr = occ_irr[number // tiles_virtual] ^ vir_irr[number % tiles_virtual]
        same = jnp.where(p_irr == k_irr, 1.0, 0.0).astype(jnp.float32)
        factor = jnp.full((TILE, TILE), same, jnp.float32).astype(jnp.bfloat16)
        here = pl.ds(tile * TILE, TILE)
        amp[:, here] = amp[:, here] * factor

    def multiply(rel, m):
        source = rows_of[rel] + m * shift
        part[rel, m] = jnp.dot(amp[...], blocks[source], preferred_element_type=jnp.float32)

    def z_unit(rel, m, s):
        d = rows_of[rel] // 2
        side = jnp.where(z > d, 1, 0)
        rows = pl.ds(s * height, height)
        unit = (rel * 2 + m) * SPLITS + s
        copy = remote(
            part.at[rel, m, rows],
            incoming.at[side, rel, m, rows],
            z_send.at[unit],
            z_recv.at[side, unit],
            (r, z + 1 - 2 * side),
        )
        upstream = jnp.where(z > d, nz - 1 - z, z)
        return d, side, rows, unit, copy, upstream

    def z_wait(side, rel, m, rows, unit):
        ref = incoming.at[side, rel, m, rows]
        remote(ref, ref, z_send.at[unit], z_recv.at[side, unit], (r, z)).wait_recv()

    def z_begin(rel, m):
        for s in range(SPLITS):
            d, side, rows, unit, copy, upstream = z_unit(rel, m, s)

            @pl.when(jnp.logical_and(z != d, upstream == 0))
            def _():
                copy.start()

    def z_middle(rel, m):
        for s in range(SPLITS):
            d, side, rows, unit, copy, upstream = z_unit(rel, m, s)

            @pl.when(jnp.logical_and(z != d, upstream > 0))
            def _():
                z_wait(side, rel, m, rows, unit)
                part[rel, m, rows] = part[rel, m, rows] + incoming[side, rel, m, rows]
                copy.start()

    def z_end(rel, m):
        for s in range(SPLITS):
            d, side, rows, unit, copy, upstream = z_unit(rel, m, s)

            @pl.when(z == d)
            def _():
                @pl.when(z > 0)
                def _():
                    z_wait(0, rel, m, rows, unit)
                    part[rel, m, rows] = part[rel, m, rows] + incoming[0, rel, m, rows]

                @pl.when(z < nz - 1)
                def _():
                    z_wait(1, rel, m, rows, unit)
                    part[rel, m, rows] = part[rel, m, rows] + incoming[1, rel, m, rows]

                side_of = core + m * shift
                here = pl.ds(pl.multiple_of(side_of * COLS, COLS), COLS)
                out_ref[rows, here] = part[rel, m, rows] * keep / denom[rows, here]

            @pl.when(z != d)
            def _():
                copy.wait_send()

    int_copy.wait()
    multiply(0, 0)
    z_begin(0, 0)
    for chunk in range(CHUNKS):
        sibling_arrival(0, chunk).wait_recv()
    multiply(0, 1)
    z_begin(0, 1)

    for i, (cx, cy) in enumerate(zip(x_order, y_order)):
        arrival(1, cx).wait_recv()
        if cx < half:
            forward(cx).start()
        to_sibling(1, cx).start()
        arrival(2, cy).wait_recv()
        if cy >= half:
            forward(cy).start()
        to_sibling(2, cy).start()
        if i == half - 1:
            z_middle(0, 0)
            z_middle(0, 1)
    for rel in (1, 2):
        multiply(rel, 0)
        z_begin(rel, 0)
    for rel in (1, 2):
        for chunk in range(CHUNKS):
            sibling_arrival(rel, chunk).wait_recv()
        multiply(rel, 1)
        z_begin(rel, 1)

    for i in range(half):
        for chunk in (i, i + half):
            arrival(3, chunk).wait_recv()
            to_sibling(3, chunk).start()
        if i < half - 1:
            for rel in (1, 2):
                for m in (0, 1):
                    z_middle(rel, m)
    multiply(3, 0)
    z_begin(3, 0)
    for chunk in range(CHUNKS):
        sibling_arrival(3, chunk).wait_recv()
    multiply(3, 1)
    z_begin(3, 1)
    for m in (0, 1):
        z_middle(3, m)
    for rel in range(4):
        for m in (0, 1):
            z_end(rel, m)

    for chunk in range(CHUNKS):
        near(0, chunk).wait_send()
        near(1, chunk).wait_send()
        forward(chunk).wait_send()
        for rel in range(4):
            to_sibling(rel, chunk).wait_send()


def fused(nz, amplitudes, integrals, occ_irrep, vir_irrep, occ_energy, vir_energy):
    rows, depth = amplitudes.shape
    smem = pl.BlockSpec(memory_space=pltpu.SMEM)
    vmem = pl.BlockSpec(memory_space=pltpu.VMEM)
    units = 8 * SPLITS
    return pl.pallas_call(
        functools.partial(cycle_kernel, nz),
        out_shape=jax.ShapeDtypeStruct((rows, TILE), jnp.float32),
        in_specs=[
            pl.BlockSpec(memory_space=pl.ANY),
            pl.BlockSpec(memory_space=pl.ANY),
            smem,
            smem,
            smem,
            vmem,
        ],
        out_specs=vmem,
        scratch_shapes=[
            pltpu.VMEM((8, depth, COLS), jnp.bfloat16),
            pltpu.VMEM((rows, depth), jnp.bfloat16),
            pltpu.VMEM((4, 2, rows, COLS), jnp.float32),
            pltpu.VMEM((2, 4, 2, rows, COLS), jnp.float32),
            pltpu.VMEM((rows, TILE), jnp.float32),
            pltpu.SemaphoreType.DMA((2,)),
            pltpu.SemaphoreType.DMA((2, CHUNKS)),
            pltpu.SemaphoreType.DMA((3, CHUNKS)),
            pltpu.SemaphoreType.DMA((CHUNKS,)),
            pltpu.SemaphoreType.DMA((4, CHUNKS)),
            pltpu.SemaphoreType.DMA((4, CHUNKS)),
            pltpu.SemaphoreType.DMA((units,)),
            pltpu.SemaphoreType.DMA((2, units)),
        ],
        compiler_params=pltpu.CompilerParams(
            collective_id=0, has_side_effects=True, vmem_limit_bytes=32 << 20
        ),
    )(
        amplitudes,
        integrals,
        occ_irrep,
        vir_irrep,
        occ_energy,
        vir_energy.reshape(1, -1),
    )


def solution(mesh):
    row, col = mesh.shape["row"], mesh.shape["col"]

    def shards(amplitudes, integrals, occ_irrep, vir_irrep, occ_energy, vir_energy):
        args = (amplitudes, integrals, occ_irrep, vir_irrep, occ_energy, vir_energy)
        plain = (
            (row, col) == (8, 4)
            and amplitudes.shape[0] == TILE
            and integrals.shape[1] == COLS
            and vir_energy.shape[0] == TILE * vir_irrep.shape[0]
        )
        return fused(col, *args) if plain else general(*args)

    return jax.shard_map(
        shards,
        mesh=mesh,
        in_specs=(P("row", "col"), P("col", "row"), P(), P(), P(), P()),
        out_specs=P("row", "col"),
        check_vma=False,
    )
```

```python
import functools

import jax
import jax.numpy as jnp
from jax import lax
from jax.experimental import pallas as pl
from jax.experimental.pallas import tpu as pltpu
from jax.sharding import PartitionSpec as P

TILE = 256
MESH = pl.DeviceIdType.MESH


def lookup(table, index):
    hits = index[:, None] == jnp.arange(table.shape[0], dtype=jnp.int32)[None, :]
    return jnp.sum(jnp.where(hits, table[None, :], jnp.zeros_like(table)[None, :]), axis=1)


def irreps(first_tile, count, occ_irrep, vir_irrep, tiles_virtual):
    tiles = first_tile + jnp.arange(count, dtype=jnp.int32)
    return jnp.bitwise_xor(
        lookup(occ_irrep, tiles // tiles_virtual), lookup(vir_irrep, tiles % tiles_virtual)
    )


def general(amplitudes, integrals, occ_irrep, vir_irrep, occ_energy, vir_energy):
    tile_size = TILE
    tiles_virtual = vir_irrep.shape[0]
    virtual_count = vir_energy.shape[0]
    p_rows, k_cols = amplitudes.shape
    p_tiles = p_rows // tile_size
    k_tiles = k_cols // tile_size
    row_index = lax.axis_index("row")
    col_index = lax.axis_index("col")
    p_irr = irreps(row_index * p_tiles, p_tiles, occ_irrep, vir_irrep, tiles_virtual)
    k_irr = irreps(col_index * k_tiles, k_tiles, occ_irrep, vir_irrep, tiles_virtual)
    match = p_irr[:, None] == k_irr[None, :]
    masked_amp = (
        amplitudes.reshape(p_tiles, tile_size, k_tiles, tile_size)
        * match[:, None, :, None].astype(jnp.bfloat16)
    ).reshape(p_rows, k_cols)
    piece = lax.all_gather(integrals, "row", axis=1, tiled=True)
    width = piece.shape[1]
    columns = jnp.arange(width, dtype=jnp.int32)
    column_tiles = columns // tile_size
    q_irr = jnp.bitwise_xor(
        lookup(occ_irrep, column_tiles // tiles_virtual),
        lookup(vir_irrep, column_tiles % tiles_virtual),
    )
    keeper = (k_irr[:, None] == q_irr[None, :]).astype(jnp.bfloat16)
    masked_int = (piece.reshape(k_tiles, tile_size, width) * keeper[:, None, :]).reshape(
        k_cols, width
    )
    partial_cycle = jnp.dot(masked_amp, masked_int, preferred_element_type=jnp.float32)
    cycle = lax.psum_scatter(partial_cycle, "col", scatter_dimension=1, tiled=True)
    q_cols = cycle.shape[1]
    row_pairs = row_index * p_rows + jnp.arange(p_rows, dtype=jnp.int32)
    col_pairs = col_index * q_cols + jnp.arange(q_cols, dtype=jnp.int32)
    row_energy = lookup(vir_energy, row_pairs % virtual_count) - lookup(
        occ_energy, row_pairs // virtual_count
    )
    col_energy = lookup(vir_energy, col_pairs % virtual_count) - lookup(
        occ_energy, col_pairs // virtual_count
    )
    return cycle / (row_energy[:, None] + col_energy[None, :])


CHUNKS = 4
COLS = 128
SLOTS = 8
TOP = 32767.0


def select_tiles(k_irr, irrep, slots):
    tiles = len(k_irr)
    found = [jnp.int32(tiles)] * slots
    count = jnp.int32(0)
    for tile in range(tiles):
        hit = k_irr[tile] == irrep
        found = [
            jnp.where(jnp.logical_and(hit, count == s), tile, found[s]) for s in range(slots)
        ]
        count = count + jnp.where(hit, 1, 0)
    return found


def cycle_kernel(
    nz,
    slots,
    amp_hbm,
    int_hbm,
    occ_irr,
    vir_irr,
    occ_e,
    vir_e,
    out_ref,
    mine,
    blocks,
    amp,
    own,
    codes,
    scales,
    in_codes,
    in_scales,
    denom,
    int_sem,
    amp_sem,
    near_send,
    near_recv,
    fwd_send,
    sib_send,
    sib_recv,
    z_send,
    z_recv,
):
    r = lax.axis_index("row")
    z = lax.axis_index("col")
    core = r % 2
    x = (r // 2) % 2
    y = r // 4
    xr = r + 2 - 4 * x
    yr = r + 4 - 8 * y
    dr = xr + yr - r
    shift = 1 - 2 * core
    sr = r + shift
    rows_of = (r, xr, yr, dr)
    tiles_virtual = vir_irr.shape[0]
    k_tiles = mine.shape[0]
    dense = slots == k_tiles
    step = slots * TILE // CHUNKS

    def remote(src, dst, send_sem, recv_sem, target):
        return pltpu.make_async_remote_copy(
            src_ref=src,
            dst_ref=dst,
            send_sem=send_sem,
            recv_sem=recv_sem,
            device_id=target,
            device_id_type=MESH,
        )

    int_copies = []
    for tile in range(k_tiles):
        here = pl.ds(tile * TILE, TILE)
        copy = pltpu.make_async_copy(int_hbm.at[here], mine.at[tile], int_sem.at[tile])
        copy.start()
        int_copies.append(copy)
    amp_copies = []
    for tile in range(k_tiles):
        here = pl.ds(tile * TILE, TILE)
        copy = pltpu.make_async_copy(amp_hbm.at[:, here], amp.at[tile], amp_sem.at[tile])
        copy.start()
        amp_copies.append(copy)

    barrier = pltpu.get_barrier_semaphore()
    for target in (xr, yr, sr):
        pl.semaphore_signal(barrier, inc=1, device_id=(target, z), device_id_type=MESH)
    for k in range(1, nz):
        pl.semaphore_signal(barrier, inc=1, device_id=(r, (z + k) % nz), device_id_type=MESH)

    def irrep(number):
        return occ_irr[number // tiles_virtual] ^ vir_irr[number % tiles_virtual]

    p_irr = irrep(r)
    q_irr = irrep(z)
    k_irr = [irrep(z * k_tiles + tile) for tile in range(k_tiles)]
    keep = jnp.where(p_irr == q_irr, 1.0, 0.0).astype(jnp.float32)
    if dense:
        chosen = [list(range(k_tiles))] * 4
    else:
        chosen = [select_tiles(k_irr, irrep(source // 2), slots) for source in rows_of]

    for copy in int_copies:
        copy.wait()
    for s in range(slots):
        tile = chosen[0][s] if dense else jnp.minimum(chosen[0][s], k_tiles - 1)
        blocks[r, pl.ds(s * TILE, TILE)] = mine[tile]

    pl.semaphore_wait(barrier, 3 + nz - 1)

    half = CHUNKS // 2
    x_order = list(range(CHUNKS))
    y_order = x_order[half:] + x_order[:half]

    def piece(source, chunk):
        return blocks.at[source, pl.ds(chunk * step, step)]

    def near(axis, chunk):
        ref = piece(r, chunk)
        return remote(
            ref, ref, near_send.at[axis, chunk], near_recv.at[axis, chunk], ((xr, yr)[axis], z)
        )

    def arrival(rel, chunk):
        ref = piece(rows_of[rel], chunk)
        return remote(ref, ref, near_send.at[0, chunk], near_recv.at[rel - 1, chunk], (xr, z))

    def forward(chunk):
        source, target = (xr, yr) if chunk < half else (yr, xr)
        ref = piece(source, chunk)
        return remote(ref, ref, fwd_send.at[chunk], near_recv.at[2, chunk], (target, z))

    def to_sibling(rel, chunk):
        ref = piece(rows_of[rel], chunk)
        return remote(ref, ref, sib_send.at[rel, chunk], sib_recv.at[rel, chunk], (sr, z))

    def sibling_arrival(rel, chunk):
        ref = piece(rows_of[rel] + shift, chunk)
        return remote(ref, ref, sib_send.at[rel, chunk], sib_recv.at[rel, chunk], (sr, z))

    for cx, cy in zip(x_order, y_order):
        near(0, cx).start()
        near(1, cy).start()
    for chunk in range(CHUNKS):
        to_sibling(0, chunk).start()

    amp[k_tiles] = jnp.zeros((TILE, TILE), jnp.bfloat16)
    for tile in range(k_tiles):
        amp_copies[tile].wait()
        same = jnp.where(p_irr == k_irr[tile], 1.0, 0.0).astype(jnp.float32)
        amp[tile] = amp[tile] * jnp.full((TILE, TILE), same, jnp.float32).astype(jnp.bfloat16)

    def code_send(rel, m, d):
        return (
            remote(
                codes.at[rel, m],
                in_codes.at[z, m],
                z_send.at[0, rel, m],
                z_recv.at[0, z, m],
                (r, d),
            ),
            remote(
                scales.at[rel, m],
                in_scales.at[z, m],
                z_send.at[1, rel, m],
                z_recv.at[1, z, m],
                (r, d),
            ),
        )

    def multiply(rel, m):
        source = rows_of[rel]
        d = source // 2
        left = jnp.concatenate([amp[tile] for tile in chosen[rel]], axis=1)
        product = jnp.dot(
            left, blocks[source + m * shift], preferred_element_type=jnp.float32
        )

        @pl.when(z == d)
        def _():
            own[m] = product

        @pl.when(z != d)
        def _():
            parts = product.reshape(TILE // 8, 8, COLS)
            most = jnp.maximum(jnp.max(jnp.abs(parts), axis=0), 1e-30)
            scales[rel, m] = most * (1.0 / TOP)
            scaled = jnp.floor(parts * (TOP / most)[None] + 0.5)
            whole = jnp.clip(scaled, -TOP, TOP).astype(jnp.int32)
            codes[rel, m] = whole.reshape(TILE, COLS).astype(jnp.int16)
            for copy in code_send(rel, m, d):
                copy.start()

    multiply(0, 0)
    for chunk in range(CHUNKS):
        sibling_arrival(0, chunk).wait_recv()
    multiply(0, 1)

    for cx, cy in zip(x_order, y_order):
        arrival(1, cx).wait_recv()
        if cx < half:
            forward(cx).start()
        to_sibling(1, cx).start()
        arrival(2, cy).wait_recv()
        if cy >= half:
            forward(cy).start()
        to_sibling(2, cy).start()
    for rel in (1, 2):
        multiply(rel, 0)
    for rel in (1, 2):
        for chunk in range(CHUNKS):
            sibling_arrival(rel, chunk).wait_recv()
        multiply(rel, 1)

    v_row = vir_e[:, pl.ds(pl.multiple_of((r % tiles_virtual) * TILE, TILE), TILE)]
    v_col = vir_e[:, pl.ds(pl.multiple_of((z % tiles_virtual) * TILE, TILE), TILE)]
    row_energy = v_row - occ_e[r // tiles_virtual]
    col_energy = v_col - occ_e[z // tiles_virtual]
    denom[...] = jnp.broadcast_to(row_energy, (TILE, TILE)).T + col_energy

    for i in range(half):
        for chunk in (i, i + half):
            arrival(3, chunk).wait_recv()
            to_sibling(3, chunk).start()
    multiply(3, 0)
    for chunk in range(CHUNKS):
        sibling_arrival(3, chunk).wait_recv()
    multiply(3, 1)

    for m in (0, 1):
        total = own[m]
        for k in range(1, nz):
            source = (z + k) % nz
            code_ref = in_codes.at[source, m]
            scale_ref = in_scales.at[source, m]
            target = (r, source)
            remote(
                code_ref, code_ref, z_send.at[0, 0, m], z_recv.at[0, source, m], target
            ).wait_recv()
            remote(
                scale_ref, scale_ref, z_send.at[1, 0, m], z_recv.at[1, source, m], target
            ).wait_recv()
            values = in_codes[source, m].astype(jnp.int32).astype(jnp.float32)
            values = values.reshape(TILE // 8, 8, COLS) * in_scales[source, m][None]
            total = total + values.reshape(TILE, COLS)
        here = pl.ds(pl.multiple_of((core + m * shift) * COLS, COLS), COLS)
        out_ref[:, here] = total * keep / denom[:, here]

    for rel in range(4):
        d = rows_of[rel] // 2

        @pl.when(z != d)
        def _():
            for m in (0, 1):
                for copy in code_send(rel, m, d):
                    copy.wait_send()

    for chunk in range(CHUNKS):
        near(0, chunk).wait_send()
        near(1, chunk).wait_send()
        forward(chunk).wait_send()
        for rel in range(4):
            to_sibling(rel, chunk).wait_send()


def fused(nz, slots, amplitudes, integrals, occ_irrep, vir_irrep, occ_energy, vir_energy):
    rows, depth = amplitudes.shape
    k_tiles = depth // TILE
    smem = pl.BlockSpec(memory_space=pltpu.SMEM)
    vmem = pl.BlockSpec(memory_space=pltpu.VMEM)
    hbm = pl.BlockSpec(memory_space=pltpu.HBM)
    dma = pltpu.SemaphoreType.DMA
    return pl.pallas_call(
        functools.partial(cycle_kernel, nz, slots),
        out_shape=jax.ShapeDtypeStruct((rows, TILE), jnp.float32),
        in_specs=[hbm, hbm, smem, smem, smem, vmem],
        out_specs=vmem,
        scratch_shapes=[
            pltpu.VMEM((k_tiles, TILE, COLS), jnp.bfloat16),
            pltpu.VMEM((8, slots * TILE, COLS), jnp.bfloat16),
            pltpu.VMEM((k_tiles + 1, rows, TILE), jnp.bfloat16),
            pltpu.VMEM((2, rows, COLS), jnp.float32),
            pltpu.VMEM((4, 2, rows, COLS), jnp.int16),
            pltpu.VMEM((4, 2, 8, COLS), jnp.float32),
            pltpu.VMEM((nz, 2, rows, COLS), jnp.int16),
            pltpu.VMEM((nz, 2, 8, COLS), jnp.float32),
            pltpu.VMEM((rows, TILE), jnp.float32),
            dma((k_tiles,)),
            dma((k_tiles,)),
            dma((2, CHUNKS)),
            dma((3, CHUNKS)),
            dma((CHUNKS,)),
            dma((4, CHUNKS)),
            dma((4, CHUNKS)),
            dma((2, 4, 2)),
            dma((2, nz, 2)),
        ],
        compiler_params=pltpu.CompilerParams(
            collective_id=slots, has_side_effects=True, vmem_limit_bytes=48 << 20
        ),
    )(amplitudes, integrals, occ_irrep, vir_irrep, occ_energy, vir_energy.reshape(1, -1))


def solution(mesh):
    row, col = mesh.shape["row"], mesh.shape["col"]

    def shards(amplitudes, integrals, occ_irrep, vir_irrep, occ_energy, vir_energy):
        args = (amplitudes, integrals, occ_irrep, vir_irrep, occ_energy, vir_energy)
        plain = (
            (row, col) == (8, 4)
            and amplitudes.shape[0] == TILE
            and integrals.shape[1] == COLS
            and vir_energy.shape[0] == TILE * vir_irrep.shape[0]
        )
        return fused(col, SLOTS, *args) if plain else general(*args)

    return jax.shard_map(
        shards,
        mesh=mesh,
        in_specs=(P("row", "col"), P("col", "row"), P(), P(), P(), P()),
        out_specs=P("row", "col"),
        check_vma=False,
    )
```

```python
import functools

import jax
import jax.numpy as jnp
from jax import lax
from jax.experimental import pallas as pl
from jax.experimental.pallas import tpu as pltpu
from jax.sharding import PartitionSpec as P

TILE = 256
MESH = pl.DeviceIdType.MESH


def lookup(table, index):
    hits = index[:, None] == jnp.arange(table.shape[0], dtype=jnp.int32)[None, :]
    return jnp.sum(jnp.where(hits, table[None, :], jnp.zeros_like(table)[None, :]), axis=1)


def irreps(first_tile, count, occ_irrep, vir_irrep, tiles_virtual):
    tiles = first_tile + jnp.arange(count, dtype=jnp.int32)
    return jnp.bitwise_xor(
        lookup(occ_irrep, tiles // tiles_virtual), lookup(vir_irrep, tiles % tiles_virtual)
    )


def general(amplitudes, integrals, occ_irrep, vir_irrep, occ_energy, vir_energy):
    tile_size = TILE
    tiles_virtual = vir_irrep.shape[0]
    virtual_count = vir_energy.shape[0]
    p_rows, k_cols = amplitudes.shape
    p_tiles = p_rows // tile_size
    k_tiles = k_cols // tile_size
    row_index = lax.axis_index("row")
    col_index = lax.axis_index("col")
    p_irr = irreps(row_index * p_tiles, p_tiles, occ_irrep, vir_irrep, tiles_virtual)
    k_irr = irreps(col_index * k_tiles, k_tiles, occ_irrep, vir_irrep, tiles_virtual)
    match = p_irr[:, None] == k_irr[None, :]
    masked_amp = (
        amplitudes.reshape(p_tiles, tile_size, k_tiles, tile_size)
        * match[:, None, :, None].astype(jnp.bfloat16)
    ).reshape(p_rows, k_cols)
    piece = lax.all_gather(integrals, "row", axis=1, tiled=True)
    width = piece.shape[1]
    columns = jnp.arange(width, dtype=jnp.int32)
    column_tiles = columns // tile_size
    q_irr = jnp.bitwise_xor(
        lookup(occ_irrep, column_tiles // tiles_virtual),
        lookup(vir_irrep, column_tiles % tiles_virtual),
    )
    keeper = (k_irr[:, None] == q_irr[None, :]).astype(jnp.bfloat16)
    masked_int = (piece.reshape(k_tiles, tile_size, width) * keeper[:, None, :]).reshape(
        k_cols, width
    )
    partial_cycle = jnp.dot(masked_amp, masked_int, preferred_element_type=jnp.float32)
    cycle = lax.psum_scatter(partial_cycle, "col", scatter_dimension=1, tiled=True)
    q_cols = cycle.shape[1]
    row_pairs = row_index * p_rows + jnp.arange(p_rows, dtype=jnp.int32)
    col_pairs = col_index * q_cols + jnp.arange(q_cols, dtype=jnp.int32)
    row_energy = lookup(vir_energy, row_pairs % virtual_count) - lookup(
        occ_energy, row_pairs // virtual_count
    )
    col_energy = lookup(vir_energy, col_pairs % virtual_count) - lookup(
        occ_energy, col_pairs // virtual_count
    )
    return cycle / (row_energy[:, None] + col_energy[None, :])


CHUNKS = 4
COLS = 128
SLOTS = (4, 5)
TOP = 32767.0


def select_tiles(k_irr, irrep, slots):
    tiles = len(k_irr)
    found = [jnp.int32(tiles)] * slots
    count = jnp.int32(0)
    for tile in range(tiles):
        hit = k_irr[tile] == irrep
        found = [
            jnp.where(jnp.logical_and(hit, count == s), tile, found[s]) for s in range(slots)
        ]
        count = count + jnp.where(hit, 1, 0)
    return found


def cycle_kernel(
    nz,
    slots,
    amp_hbm,
    int_hbm,
    occ_irr,
    vir_irr,
    occ_e,
    vir_e,
    out_ref,
    mine,
    blocks,
    amp,
    own,
    codes,
    scales,
    in_codes,
    in_scales,
    denom,
    int_sem,
    amp_sem,
    near_send,
    near_recv,
    fwd_send,
    sib_send,
    sib_recv,
    z_send,
    z_recv,
):
    r = lax.axis_index("row")
    z = lax.axis_index("col")
    core = r % 2
    x = (r // 2) % 2
    y = r // 4
    xr = r + 2 - 4 * x
    yr = r + 4 - 8 * y
    dr = xr + yr - r
    shift = 1 - 2 * core
    sr = r + shift
    rows_of = (r, xr, yr, dr)
    tiles_virtual = vir_irr.shape[0]
    k_tiles = mine.shape[0]
    dense = slots == k_tiles
    step = slots * TILE // CHUNKS

    def remote(src, dst, send_sem, recv_sem, target):
        return pltpu.make_async_remote_copy(
            src_ref=src,
            dst_ref=dst,
            send_sem=send_sem,
            recv_sem=recv_sem,
            device_id=target,
            device_id_type=MESH,
        )

    int_copies = []
    for tile in range(k_tiles):
        here = pl.ds(tile * TILE, TILE)
        copy = pltpu.make_async_copy(int_hbm.at[here], mine.at[tile], int_sem.at[tile])
        copy.start()
        int_copies.append(copy)
    amp_copies = []
    for tile in range(k_tiles):
        here = pl.ds(tile * TILE, TILE)
        copy = pltpu.make_async_copy(amp_hbm.at[:, here], amp.at[tile], amp_sem.at[tile])
        copy.start()
        amp_copies.append(copy)

    barrier = pltpu.get_barrier_semaphore()
    for target in (xr, yr, sr):
        pl.semaphore_signal(barrier, inc=1, device_id=(target, z), device_id_type=MESH)
    for k in range(1, nz):
        pl.semaphore_signal(barrier, inc=1, device_id=(r, (z + k) % nz), device_id_type=MESH)

    def irrep(number):
        return occ_irr[number // tiles_virtual] ^ vir_irr[number % tiles_virtual]

    p_irr = irrep(r)
    q_irr = irrep(z)
    k_irr = [irrep(z * k_tiles + tile) for tile in range(k_tiles)]
    keep = jnp.where(p_irr == q_irr, 1.0, 0.0).astype(jnp.float32)
    if dense:
        chosen = [list(range(k_tiles))] * 4
    else:
        chosen = [select_tiles(k_irr, irrep(source // 2), slots) for source in rows_of]

    for copy in int_copies:
        copy.wait()
    for s in range(slots):
        tile = chosen[0][s] if dense else jnp.minimum(chosen[0][s], k_tiles - 1)
        blocks[r, pl.ds(s * TILE, TILE)] = mine[tile]

    pl.semaphore_wait(barrier, 3 + nz - 1)

    half = CHUNKS // 2
    x_order = list(range(CHUNKS))
    y_order = x_order[half:] + x_order[:half]

    def piece(source, chunk):
        return blocks.at[source, pl.ds(chunk * step, step)]

    def near(axis, chunk):
        ref = piece(r, chunk)
        return remote(
            ref, ref, near_send.at[axis, chunk], near_recv.at[axis, chunk], ((xr, yr)[axis], z)
        )

    def arrival(rel, chunk):
        ref = piece(rows_of[rel], chunk)
        return remote(ref, ref, near_send.at[0, chunk], near_recv.at[rel - 1, chunk], (xr, z))

    def forward(chunk):
        source, target = (xr, yr) if chunk < half else (yr, xr)
        ref = piece(source, chunk)
        return remote(ref, ref, fwd_send.at[chunk], near_recv.at[2, chunk], (target, z))

    def to_sibling(rel, chunk):
        ref = piece(rows_of[rel], chunk)
        return remote(ref, ref, sib_send.at[rel, chunk], sib_recv.at[rel, chunk], (sr, z))

    def sibling_arrival(rel, chunk):
        ref = piece(rows_of[rel] + shift, chunk)
        return remote(ref, ref, sib_send.at[rel, chunk], sib_recv.at[rel, chunk], (sr, z))

    for cx, cy in zip(x_order, y_order):
        near(0, cx).start()
        near(1, cy).start()
    for chunk in range(CHUNKS):
        to_sibling(0, chunk).start()

    amp[k_tiles] = jnp.zeros((TILE, TILE), jnp.bfloat16)
    for tile in range(k_tiles):
        amp_copies[tile].wait()
        same = jnp.where(p_irr == k_irr[tile], 1.0, 0.0).astype(jnp.float32)
        amp[tile] = amp[tile] * jnp.full((TILE, TILE), same, jnp.float32).astype(jnp.bfloat16)

    def code_send(rel, m, d):
        return (
            remote(
                codes.at[rel, m],
                in_codes.at[z, m],
                z_send.at[0, rel, m],
                z_recv.at[0, z, m],
                (r, d),
            ),
            remote(
                scales.at[rel, m],
                in_scales.at[z, m],
                z_send.at[1, rel, m],
                z_recv.at[1, z, m],
                (r, d),
            ),
        )

    def multiply(rel, m):
        source = rows_of[rel]
        d = source // 2
        left = jnp.concatenate([amp[tile] for tile in chosen[rel]], axis=1)
        product = jnp.dot(
            left, blocks[source + m * shift], preferred_element_type=jnp.float32
        )

        @pl.when(z == d)
        def _():
            own[m] = product

        @pl.when(z != d)
        def _():
            parts = product.reshape(TILE // 8, 8, COLS)
            most = jnp.maximum(jnp.max(jnp.abs(parts), axis=0), 1e-30)
            scales[rel, m] = most * (1.0 / TOP)
            scaled = jnp.floor(parts * (TOP / most)[None] + 0.5)
            whole = jnp.clip(scaled, -TOP, TOP).astype(jnp.int32)
            codes[rel, m] = whole.reshape(TILE, COLS).astype(jnp.int16)
            for copy in code_send(rel, m, d):
                copy.start()

    multiply(0, 0)
    for chunk in range(CHUNKS):
        sibling_arrival(0, chunk).wait_recv()
    multiply(0, 1)

    for cx, cy in zip(x_order, y_order):
        arrival(1, cx).wait_recv()
        if cx < half:
            forward(cx).start()
        to_sibling(1, cx).start()
        arrival(2, cy).wait_recv()
        if cy >= half:
            forward(cy).start()
        to_sibling(2, cy).start()
    for rel in (1, 2):
        multiply(rel, 0)
    for rel in (1, 2):
        for chunk in range(CHUNKS):
            sibling_arrival(rel, chunk).wait_recv()
        multiply(rel, 1)

    v_row = vir_e[:, pl.ds(pl.multiple_of((r % tiles_virtual) * TILE, TILE), TILE)]
    v_col = vir_e[:, pl.ds(pl.multiple_of((z % tiles_virtual) * TILE, TILE), TILE)]
    row_energy = v_row - occ_e[r // tiles_virtual]
    col_energy = v_col - occ_e[z // tiles_virtual]
    denom[...] = jnp.broadcast_to(row_energy, (TILE, TILE)).T + col_energy

    for i in range(half):
        for chunk in (i, i + half):
            arrival(3, chunk).wait_recv()
            to_sibling(3, chunk).start()
    multiply(3, 0)
    for chunk in range(CHUNKS):
        sibling_arrival(3, chunk).wait_recv()
    multiply(3, 1)

    for m in (0, 1):
        total = own[m]
        for k in range(1, nz):
            source = (z + k) % nz
            code_ref = in_codes.at[source, m]
            scale_ref = in_scales.at[source, m]
            target = (r, source)
            remote(
                code_ref, code_ref, z_send.at[0, 0, m], z_recv.at[0, source, m], target
            ).wait_recv()
            remote(
                scale_ref, scale_ref, z_send.at[1, 0, m], z_recv.at[1, source, m], target
            ).wait_recv()
            values = in_codes[source, m].astype(jnp.int32).astype(jnp.float32)
            values = values.reshape(TILE // 8, 8, COLS) * in_scales[source, m][None]
            total = total + values.reshape(TILE, COLS)
        here = pl.ds(pl.multiple_of((core + m * shift) * COLS, COLS), COLS)
        out_ref[:, here] = total * keep / denom[:, here]

    for rel in range(4):
        d = rows_of[rel] // 2

        @pl.when(z != d)
        def _():
            for m in (0, 1):
                for copy in code_send(rel, m, d):
                    copy.wait_send()

    for chunk in range(CHUNKS):
        near(0, chunk).wait_send()
        near(1, chunk).wait_send()
        forward(chunk).wait_send()
        for rel in range(4):
            to_sibling(rel, chunk).wait_send()


def fused(nz, slots, amplitudes, integrals, occ_irrep, vir_irrep, occ_energy, vir_energy):
    rows, depth = amplitudes.shape
    k_tiles = depth // TILE
    smem = pl.BlockSpec(memory_space=pltpu.SMEM)
    vmem = pl.BlockSpec(memory_space=pltpu.VMEM)
    hbm = pl.BlockSpec(memory_space=pltpu.HBM)
    dma = pltpu.SemaphoreType.DMA
    return pl.pallas_call(
        functools.partial(cycle_kernel, nz, slots),
        out_shape=jax.ShapeDtypeStruct((rows, TILE), jnp.float32),
        in_specs=[hbm, hbm, smem, smem, smem, vmem],
        out_specs=vmem,
        scratch_shapes=[
            pltpu.VMEM((k_tiles, TILE, COLS), jnp.bfloat16),
            pltpu.VMEM((8, slots * TILE, COLS), jnp.bfloat16),
            pltpu.VMEM((k_tiles + 1, rows, TILE), jnp.bfloat16),
            pltpu.VMEM((2, rows, COLS), jnp.float32),
            pltpu.VMEM((4, 2, rows, COLS), jnp.int16),
            pltpu.VMEM((4, 2, 8, COLS), jnp.float32),
            pltpu.VMEM((nz, 2, rows, COLS), jnp.int16),
            pltpu.VMEM((nz, 2, 8, COLS), jnp.float32),
            pltpu.VMEM((rows, TILE), jnp.float32),
            dma((k_tiles,)),
            dma((k_tiles,)),
            dma((2, CHUNKS)),
            dma((3, CHUNKS)),
            dma((CHUNKS,)),
            dma((4, CHUNKS)),
            dma((4, CHUNKS)),
            dma((2, 4, 2)),
            dma((2, nz, 2)),
        ],
        compiler_params=pltpu.CompilerParams(
            collective_id=slots, has_side_effects=True, vmem_limit_bytes=48 << 20
        ),
    )(amplitudes, integrals, occ_irrep, vir_irrep, occ_energy, vir_energy.reshape(1, -1))


def need_kernel(nz, k_tiles, occ_irr, vir_irr, need):
    tiles_virtual = vir_irr.shape[0]

    def irrep(number):
        return occ_irr[number // tiles_virtual] ^ vir_irr[number % tiles_virtual]

    q_irr = [irrep(number) for number in range(nz)]
    worst = jnp.int32(0)
    for part in range(nz):
        k_irr = [irrep(part * k_tiles + tile) for tile in range(k_tiles)]
        for q in range(nz):
            count = jnp.int32(0)
            for tile in range(k_tiles):
                count = count + jnp.where(k_irr[tile] == q_irr[q], 1, 0)
            worst = jnp.maximum(worst, count)
    need[0] = worst


def block_sparse(nz, *args):
    k_tiles = args[0].shape[1] // TILE
    smem = pl.BlockSpec(memory_space=pltpu.SMEM)
    need = pl.pallas_call(
        functools.partial(need_kernel, nz, k_tiles),
        out_shape=jax.ShapeDtypeStruct((1,), jnp.int32),
        in_specs=[smem, smem],
        out_specs=smem,
    )(args[2], args[3])[0]
    which = sum((need > slots).astype(jnp.int32) for slots in SLOTS)
    branches = [functools.partial(fused, nz, slots) for slots in (*SLOTS, k_tiles)]
    return lax.switch(which, branches, *args)


def solution(mesh):
    row, col = mesh.shape["row"], mesh.shape["col"]

    def shards(amplitudes, integrals, occ_irrep, vir_irrep, occ_energy, vir_energy):
        args = (amplitudes, integrals, occ_irrep, vir_irrep, occ_energy, vir_energy)
        plain = (
            (row, col) == (8, 4)
            and amplitudes.shape[0] == TILE
            and integrals.shape[1] == COLS
            and vir_energy.shape[0] == TILE * vir_irrep.shape[0]
        )
        return block_sparse(col, *args) if plain else general(*args)

    return jax.shard_map(
        shards,
        mesh=mesh,
        in_specs=(P("row", "col"), P("col", "row"), P(), P(), P(), P()),
        out_specs=P("row", "col"),
        check_vma=False,
    )
```

```python
import functools

import jax
import jax.numpy as jnp
from jax import lax
from jax.experimental import pallas as pl
from jax.experimental.pallas import tpu as pltpu
from jax.sharding import PartitionSpec as P

TILE = 256
MESH = pl.DeviceIdType.MESH


def lookup(table, index):
    hits = index[:, None] == jnp.arange(table.shape[0], dtype=jnp.int32)[None, :]
    return jnp.sum(jnp.where(hits, table[None, :], jnp.zeros_like(table)[None, :]), axis=1)


def irreps(first_tile, count, occ_irrep, vir_irrep, tiles_virtual):
    tiles = first_tile + jnp.arange(count, dtype=jnp.int32)
    return jnp.bitwise_xor(
        lookup(occ_irrep, tiles // tiles_virtual), lookup(vir_irrep, tiles % tiles_virtual)
    )


def general(amplitudes, integrals, occ_irrep, vir_irrep, occ_energy, vir_energy):
    tile_size = TILE
    tiles_virtual = vir_irrep.shape[0]
    virtual_count = vir_energy.shape[0]
    p_rows, k_cols = amplitudes.shape
    p_tiles = p_rows // tile_size
    k_tiles = k_cols // tile_size
    row_index = lax.axis_index("row")
    col_index = lax.axis_index("col")
    p_irr = irreps(row_index * p_tiles, p_tiles, occ_irrep, vir_irrep, tiles_virtual)
    k_irr = irreps(col_index * k_tiles, k_tiles, occ_irrep, vir_irrep, tiles_virtual)
    match = p_irr[:, None] == k_irr[None, :]
    masked_amp = (
        amplitudes.reshape(p_tiles, tile_size, k_tiles, tile_size)
        * match[:, None, :, None].astype(jnp.bfloat16)
    ).reshape(p_rows, k_cols)
    piece = lax.all_gather(integrals, "row", axis=1, tiled=True)
    width = piece.shape[1]
    columns = jnp.arange(width, dtype=jnp.int32)
    column_tiles = columns // tile_size
    q_irr = jnp.bitwise_xor(
        lookup(occ_irrep, column_tiles // tiles_virtual),
        lookup(vir_irrep, column_tiles % tiles_virtual),
    )
    keeper = (k_irr[:, None] == q_irr[None, :]).astype(jnp.bfloat16)
    masked_int = (piece.reshape(k_tiles, tile_size, width) * keeper[:, None, :]).reshape(
        k_cols, width
    )
    partial_cycle = jnp.dot(masked_amp, masked_int, preferred_element_type=jnp.float32)
    cycle = lax.psum_scatter(partial_cycle, "col", scatter_dimension=1, tiled=True)
    q_cols = cycle.shape[1]
    row_pairs = row_index * p_rows + jnp.arange(p_rows, dtype=jnp.int32)
    col_pairs = col_index * q_cols + jnp.arange(q_cols, dtype=jnp.int32)
    row_energy = lookup(vir_energy, row_pairs % virtual_count) - lookup(
        occ_energy, row_pairs // virtual_count
    )
    col_energy = lookup(vir_energy, col_pairs % virtual_count) - lookup(
        occ_energy, col_pairs // virtual_count
    )
    return cycle / (row_energy[:, None] + col_energy[None, :])


CHUNKS = 4
COLS = 128
SLOTS = (3, 4, 5)
TOP = 32767.0


def select_tiles(k_irr, irrep, slots):
    tiles = len(k_irr)
    found = [jnp.int32(tiles)] * slots
    count = jnp.int32(0)
    for tile in range(tiles):
        hit = k_irr[tile] == irrep
        found = [
            jnp.where(jnp.logical_and(hit, count == s), tile, found[s]) for s in range(slots)
        ]
        count = count + jnp.where(hit, 1, 0)
    return found


def cycle_kernel(
    nz,
    slots,
    amp_hbm,
    int_hbm,
    occ_irr,
    vir_irr,
    occ_e,
    vir_e,
    out_ref,
    mine,
    blocks,
    amp,
    own,
    codes,
    scales,
    in_codes,
    in_scales,
    denom,
    int_sem,
    amp_sem,
    near_send,
    near_recv,
    fwd_send,
    sib_send,
    sib_recv,
    z_send,
    z_recv,
):
    r = lax.axis_index("row")
    z = lax.axis_index("col")
    core = r % 2
    x = (r // 2) % 2
    y = r // 4
    xr = r + 2 - 4 * x
    yr = r + 4 - 8 * y
    dr = xr + yr - r
    shift = 1 - 2 * core
    sr = r + shift
    rows_of = (r, xr, yr, dr)
    tiles_virtual = vir_irr.shape[0]
    k_tiles = mine.shape[0]
    dense = slots == k_tiles
    step = slots * TILE // CHUNKS

    def remote(src, dst, send_sem, recv_sem, target):
        return pltpu.make_async_remote_copy(
            src_ref=src,
            dst_ref=dst,
            send_sem=send_sem,
            recv_sem=recv_sem,
            device_id=target,
            device_id_type=MESH,
        )

    int_copies = []
    for tile in range(k_tiles):
        here = pl.ds(tile * TILE, TILE)
        copy = pltpu.make_async_copy(int_hbm.at[here], mine.at[tile], int_sem.at[tile])
        copy.start()
        int_copies.append(copy)
    amp_copies = []
    for tile in range(k_tiles):
        here = pl.ds(tile * TILE, TILE)
        copy = pltpu.make_async_copy(amp_hbm.at[:, here], amp.at[tile], amp_sem.at[tile])
        copy.start()
        amp_copies.append(copy)

    barrier = pltpu.get_barrier_semaphore()
    for target in (xr, yr, sr):
        pl.semaphore_signal(barrier, inc=1, device_id=(target, z), device_id_type=MESH)
    for k in range(1, nz):
        pl.semaphore_signal(barrier, inc=1, device_id=(r, (z + k) % nz), device_id_type=MESH)

    def irrep(number):
        return occ_irr[number // tiles_virtual] ^ vir_irr[number % tiles_virtual]

    p_irr = irrep(r)
    q_irr = irrep(z)
    k_irr = [irrep(z * k_tiles + tile) for tile in range(k_tiles)]
    keep = jnp.where(p_irr == q_irr, 1.0, 0.0).astype(jnp.float32)
    if dense:
        chosen = [list(range(k_tiles))] * 4
    else:
        chosen = [select_tiles(k_irr, irrep(source // 2), slots) for source in rows_of]

    for copy in int_copies:
        copy.wait()
    for s in range(slots):
        tile = chosen[0][s] if dense else jnp.minimum(chosen[0][s], k_tiles - 1)
        blocks[r, pl.ds(s * TILE, TILE)] = mine[tile]

    pl.semaphore_wait(barrier, 3 + nz - 1)

    half = CHUNKS // 2
    x_order = list(range(CHUNKS))
    y_order = x_order[half:] + x_order[:half]

    def piece(source, chunk):
        return blocks.at[source, pl.ds(chunk * step, step)]

    def near(axis, chunk):
        ref = piece(r, chunk)
        return remote(
            ref, ref, near_send.at[axis, chunk], near_recv.at[axis, chunk], ((xr, yr)[axis], z)
        )

    def arrival(rel, chunk):
        ref = piece(rows_of[rel], chunk)
        return remote(ref, ref, near_send.at[0, chunk], near_recv.at[rel - 1, chunk], (xr, z))

    def forward(chunk):
        source, target = (xr, yr) if chunk < half else (yr, xr)
        ref = piece(source, chunk)
        return remote(ref, ref, fwd_send.at[chunk], near_recv.at[2, chunk], (target, z))

    def to_sibling(rel, chunk):
        ref = piece(rows_of[rel], chunk)
        return remote(ref, ref, sib_send.at[rel, chunk], sib_recv.at[rel, chunk], (sr, z))

    def sibling_arrival(rel, chunk):
        ref = piece(rows_of[rel] + shift, chunk)
        return remote(ref, ref, sib_send.at[rel, chunk], sib_recv.at[rel, chunk], (sr, z))

    for cx, cy in zip(x_order, y_order):
        near(0, cx).start()
        near(1, cy).start()
    for chunk in range(CHUNKS):
        to_sibling(0, chunk).start()

    amp[k_tiles] = jnp.zeros((TILE, TILE), jnp.bfloat16)
    for tile in range(k_tiles):
        amp_copies[tile].wait()
        same = jnp.where(p_irr == k_irr[tile], 1.0, 0.0).astype(jnp.float32)
        amp[tile] = amp[tile] * jnp.full((TILE, TILE), same, jnp.float32).astype(jnp.bfloat16)

    def code_send(rel, m, d):
        return (
            remote(
                codes.at[rel, m],
                in_codes.at[z, m],
                z_send.at[0, rel, m],
                z_recv.at[0, z, m],
                (r, d),
            ),
            remote(
                scales.at[rel, m],
                in_scales.at[z, m],
                z_send.at[1, rel, m],
                z_recv.at[1, z, m],
                (r, d),
            ),
        )

    def multiply(rel, m):
        source = rows_of[rel]
        d = source // 2
        left = jnp.concatenate([amp[tile] for tile in chosen[rel]], axis=1)
        product = jnp.dot(
            left, blocks[source + m * shift], preferred_element_type=jnp.float32
        )

        @pl.when(z == d)
        def _():
            own[m] = product

        @pl.when(z != d)
        def _():
            parts = product.reshape(TILE // 8, 8, COLS)
            most = jnp.maximum(jnp.max(jnp.abs(parts), axis=0), 1e-30)
            scales[rel, m] = most * (1.0 / TOP)
            scaled = jnp.floor(parts * (TOP / most)[None] + 0.5)
            whole = jnp.clip(scaled, -TOP, TOP).astype(jnp.int32)
            codes[rel, m] = whole.reshape(TILE, COLS).astype(jnp.int16)
            for copy in code_send(rel, m, d):
                copy.start()

    multiply(0, 0)
    for chunk in range(CHUNKS):
        sibling_arrival(0, chunk).wait_recv()
    multiply(0, 1)

    for cx, cy in zip(x_order, y_order):
        arrival(1, cx).wait_recv()
        if cx < half:
            forward(cx).start()
        to_sibling(1, cx).start()
        arrival(2, cy).wait_recv()
        if cy >= half:
            forward(cy).start()
        to_sibling(2, cy).start()
    for rel in (1, 2):
        multiply(rel, 0)
    for rel in (1, 2):
        for chunk in range(CHUNKS):
            sibling_arrival(rel, chunk).wait_recv()
        multiply(rel, 1)

    v_row = vir_e[:, pl.ds(pl.multiple_of((r % tiles_virtual) * TILE, TILE), TILE)]
    v_col = vir_e[:, pl.ds(pl.multiple_of((z % tiles_virtual) * TILE, TILE), TILE)]
    row_energy = v_row - occ_e[r // tiles_virtual]
    col_energy = v_col - occ_e[z // tiles_virtual]
    denom[...] = jnp.broadcast_to(row_energy, (TILE, TILE)).T + col_energy

    for i in range(half):
        for chunk in (i, i + half):
            arrival(3, chunk).wait_recv()
            to_sibling(3, chunk).start()
    multiply(3, 0)
    for chunk in range(CHUNKS):
        sibling_arrival(3, chunk).wait_recv()
    multiply(3, 1)

    for m in (0, 1):
        total = own[m]
        for k in range(1, nz):
            source = (z + k) % nz
            code_ref = in_codes.at[source, m]
            scale_ref = in_scales.at[source, m]
            target = (r, source)
            remote(
                code_ref, code_ref, z_send.at[0, 0, m], z_recv.at[0, source, m], target
            ).wait_recv()
            remote(
                scale_ref, scale_ref, z_send.at[1, 0, m], z_recv.at[1, source, m], target
            ).wait_recv()
            values = in_codes[source, m].astype(jnp.int32).astype(jnp.float32)
            values = values.reshape(TILE // 8, 8, COLS) * in_scales[source, m][None]
            total = total + values.reshape(TILE, COLS)
        here = pl.ds(pl.multiple_of((core + m * shift) * COLS, COLS), COLS)
        out_ref[:, here] = total * keep / denom[:, here]

    for rel in range(4):
        d = rows_of[rel] // 2

        @pl.when(z != d)
        def _():
            for m in (0, 1):
                for copy in code_send(rel, m, d):
                    copy.wait_send()

    for chunk in range(CHUNKS):
        near(0, chunk).wait_send()
        near(1, chunk).wait_send()
        forward(chunk).wait_send()
        for rel in range(4):
            to_sibling(rel, chunk).wait_send()


def fused(nz, slots, amplitudes, integrals, occ_irrep, vir_irrep, occ_energy, vir_energy):
    rows, depth = amplitudes.shape
    k_tiles = depth // TILE
    smem = pl.BlockSpec(memory_space=pltpu.SMEM)
    vmem = pl.BlockSpec(memory_space=pltpu.VMEM)
    hbm = pl.BlockSpec(memory_space=pltpu.HBM)
    dma = pltpu.SemaphoreType.DMA
    return pl.pallas_call(
        functools.partial(cycle_kernel, nz, slots),
        out_shape=jax.ShapeDtypeStruct((rows, TILE), jnp.float32),
        in_specs=[hbm, hbm, smem, smem, smem, vmem],
        out_specs=vmem,
        scratch_shapes=[
            pltpu.VMEM((k_tiles, TILE, COLS), jnp.bfloat16),
            pltpu.VMEM((8, slots * TILE, COLS), jnp.bfloat16),
            pltpu.VMEM((k_tiles + 1, rows, TILE), jnp.bfloat16),
            pltpu.VMEM((2, rows, COLS), jnp.float32),
            pltpu.VMEM((4, 2, rows, COLS), jnp.int16),
            pltpu.VMEM((4, 2, 8, COLS), jnp.float32),
            pltpu.VMEM((nz, 2, rows, COLS), jnp.int16),
            pltpu.VMEM((nz, 2, 8, COLS), jnp.float32),
            pltpu.VMEM((rows, TILE), jnp.float32),
            dma((k_tiles,)),
            dma((k_tiles,)),
            dma((2, CHUNKS)),
            dma((3, CHUNKS)),
            dma((CHUNKS,)),
            dma((4, CHUNKS)),
            dma((4, CHUNKS)),
            dma((2, 4, 2)),
            dma((2, nz, 2)),
        ],
        compiler_params=pltpu.CompilerParams(
            collective_id=slots, has_side_effects=True, vmem_limit_bytes=48 << 20
        ),
    )(amplitudes, integrals, occ_irrep, vir_irrep, occ_energy, vir_energy.reshape(1, -1))


def need_kernel(nz, k_tiles, occ_irr, vir_irr, need):
    tiles_virtual = vir_irr.shape[0]

    def irrep(number):
        return occ_irr[number // tiles_virtual] ^ vir_irr[number % tiles_virtual]

    q_irr = [irrep(number) for number in range(nz)]
    worst = jnp.int32(0)
    for part in range(nz):
        k_irr = [irrep(part * k_tiles + tile) for tile in range(k_tiles)]
        for q in range(nz):
            count = jnp.int32(0)
            for tile in range(k_tiles):
                count = count + jnp.where(k_irr[tile] == q_irr[q], 1, 0)
            worst = jnp.maximum(worst, count)
    need[0] = worst


def block_sparse(nz, *args):
    k_tiles = args[0].shape[1] // TILE
    smem = pl.BlockSpec(memory_space=pltpu.SMEM)
    need = pl.pallas_call(
        functools.partial(need_kernel, nz, k_tiles),
        out_shape=jax.ShapeDtypeStruct((1,), jnp.int32),
        in_specs=[smem, smem],
        out_specs=smem,
    )(args[2], args[3])[0]
    which = sum((need > slots).astype(jnp.int32) for slots in SLOTS)
    branches = [functools.partial(fused, nz, slots) for slots in (*SLOTS, k_tiles)]
    return lax.switch(which, branches, *args)


def solution(mesh):
    row, col = mesh.shape["row"], mesh.shape["col"]

    def shards(amplitudes, integrals, occ_irrep, vir_irrep, occ_energy, vir_energy):
        args = (amplitudes, integrals, occ_irrep, vir_irrep, occ_energy, vir_energy)
        plain = (
            (row, col) == (8, 4)
            and amplitudes.shape[0] == TILE
            and integrals.shape[1] == COLS
            and vir_energy.shape[0] == TILE * vir_irrep.shape[0]
        )
        return block_sparse(col, *args) if plain else general(*args)

    return jax.shard_map(
        shards,
        mesh=mesh,
        in_specs=(P("row", "col"), P("col", "row"), P(), P(), P(), P()),
        out_specs=P("row", "col"),
        check_vma=False,
    )
```
